32 devices in a mesh: ctx: 8 (over z, x), head: 4 (over y, core).
Axes of the slice: x: 2, y: 2, z: 4, core: 2. Of those that a mesh axis runs over, the one named last changes fastest.
Arguments:
- query_rows: bfloat16 [1536, 4096], P('ctx', 'head'), may hold values from -4.5 to 4.5
- key_rows: bfloat16 [1536, 512], P('ctx'), may hold values from -4.5 to 4.5
- value_rows: bfloat16 [1536, 512], P('ctx'), may hold values from -6 to 6
- w_out: bfloat16 [4096, 2048], P('head'), may hold values from -0.09375 to 0.09375
Outputs:
- mixed: bfloat16 [1536, 2048], P('ctx', 'head')
The draws below stay inside these ranges and needn't reach their ends.
All inputs are finite; a program needn't handle non-finite values.
Results may differ from the reference program's by a relative error of at most 0.019.
Values may be sent and summed in bfloat16 or wider, within the bound.
No kernel may reach another device: no remote copies, remote signals or barrier semaphores. Data moves between devices by JAX's collectives and lax.ppermute only.
A program may use at most 64 MiB of HBM per device.

```python
import math
import jax
import jax.numpy as jnp
from jax import lax

D = 2048
HQ = 32
KVH = 4
HD = 128
TOK_DEV = 192
TOKENS = 1536


clip_bound = 4.5


def draw_query_rows(key, part):
    sample = jax.random.normal(jax.random.fold_in(key, 1), (TOKENS, HQ * HD), jnp.float32)
    return jnp.clip(sample, -clip_bound, clip_bound).astype(jnp.bfloat16)


def draw_key_rows(key, part):
    sample = jax.random.normal(jax.random.fold_in(key, 2), (TOKENS, KVH * HD), jnp.float32)
    return jnp.clip(sample, -clip_bound, clip_bound).astype(jnp.bfloat16)


def level_of(key, dims, pieces, smallest, largest):
    def one(axis_at, shards_of):
        heights = jax.random.uniform(jax.random.fold_in(jax.random.fold_in(key, 6), axis_at), (shards_of,), jnp.float32, smallest / len(pieces), largest / len(pieces))
        return jnp.repeat(jnp.exp(heights), dims[axis_at] // shards_of).reshape((-1,) + (1,) * (len(dims) - axis_at - 1))

    gain = one(*pieces[0])
    for cut in pieces[1:]:
        gain = gain * one(*cut)
    return gain


def centred(stream_key, dims, scale, bound, pieces=(), kind=jnp.bfloat16):
    result = jax.random.normal(stream_key, dims, jnp.float32) * scale
    if len(pieces) > 0:
        result = level_of(stream_key, dims, pieces, -0.22, 0.18) * result
    return jnp.clip(result, min=-bound, max=bound).astype(kind)


def setup_inputs(seed: int = 0) -> dict:
    splits = jax.random.split(jax.random.key(seed), 5)
    query_rows = draw_query_rows(jax.random.fold_in(splits[4], 71), 0)
    key_rows = draw_key_rows(jax.random.fold_in(splits[4], 71), 0)
    value_rows = centred(splits[2], (TOKENS, KVH * HD), 1.0, 6.0, ((0, 8),))
    w_out = centred(splits[3], (HQ * HD, D), (HQ * HD) ** -0.5, 0.09375, ((0, 4),))
    return {"query_rows": query_rows, "key_rows": key_rows, "value_rows": value_rows, "w_out": w_out}


def reference(query_rows, key_rows, value_rows, w_out):
    tokens_all = query_rows.shape[0]
    group_size = HQ // KVH
    score_scale = 1.0 / math.sqrt(HD)
    grouped = query_rows.reshape(tokens_all, KVH, group_size, HD)
    key_heads = key_rows.astype(jnp.float32).reshape(tokens_all, KVH, HD)
    value_heads = value_rows.astype(jnp.float32).reshape(tokens_all, KVH, HD)
    key_positions = jnp.arange(tokens_all, dtype=jnp.int32)

    def one_block(block_number):
        first_row = block_number * TOK_DEV
        block_queries = lax.dynamic_slice_in_dim(grouped, first_row, TOK_DEV, 0).astype(jnp.float32)
        scores = jnp.einsum('tgjd,sgd->gjts', block_queries, key_heads) * score_scale
        query_positions = first_row + jnp.arange(TOK_DEV, dtype=jnp.int32)
        allowed = key_positions[None, :] <= query_positions[:, None]
        scores = jnp.where(allowed, scores, -1e+30)
        maximum = lax.optimization_barrier(jnp.max(scores, axis=3, keepdims=True))
        raised = jnp.where(allowed, jnp.exp(scores - maximum), 0.0)
        denominator = lax.optimization_barrier(jnp.sum(raised, axis=3))
        rounded = lax.optimization_barrier(raised.astype(jnp.bfloat16))
        weights = rounded.astype(jnp.float32)
        numerator = jnp.einsum('gjts,sgd->tgjd', weights, value_heads)
        scaled = numerator / jnp.transpose(denominator, (2, 0, 1))[:, :, :, None]
        return scaled.astype(jnp.bfloat16).reshape(TOK_DEV, HQ * HD)
    blocks = lax.map(one_block, jnp.arange(tokens_all // TOK_DEV, dtype=jnp.int32))
    attended = blocks.reshape(tokens_all, HQ * HD)
    return jnp.dot(attended, w_out, preferred_element_type=jnp.float32).astype(jnp.bfloat16)
```

```python
import functools
import math

import jax
import jax.numpy as jnp
from jax import lax
from jax.experimental import pallas as pl
from jax.experimental.pallas import tpu as pltpu
from jax.sharding import PartitionSpec as P

KVH = 4
HD = 128

NEGATIVE = -1e30
EXP2_SCALE = math.log2(math.e) / math.sqrt(HD)


VMEM = pl.BlockSpec(memory_space=pltpu.VMEM)
SMEM = pl.BlockSpec(memory_space=pltpu.SMEM)
HBM = pl.BlockSpec(memory_space=pl.ANY)


def chunk_of(rows):
    return 256 if rows % 256 == 0 else 128 if rows % 128 == 0 else rows


def pick_kernel(head_ref, key_ref, value_ref, out_ref, sems):
    column = pl.multiple_of(head_ref[0] * HD, HD)
    copies = [
        pltpu.make_async_copy(
            ref.at[:, pl.ds(column, HD)], out_ref.at[:, pl.ds(i * HD, HD)], sems.at[i]
        )
        for i, ref in enumerate((key_ref, value_ref))
    ]
    for copy in copies:
        copy.start()
    for copy in copies:
        copy.wait()


def pick(kv_head, key_rows, value_rows):
    tokens = key_rows.shape[0]
    return pl.pallas_call(
        pick_kernel,
        out_shape=jax.ShapeDtypeStruct((tokens, 2 * HD), key_rows.dtype),
        in_specs=[SMEM, HBM, HBM],
        out_specs=VMEM,
        scratch_shapes=[pltpu.SemaphoreType.DMA((2,))],
        cost_estimate=pl.CostEstimate(flops=0, bytes_accessed=4 * tokens * HD * 2, transcendentals=0),
        name="pick",
    )(kv_head, key_rows, value_rows)


def add_block(kv_ref, queries_ref, highest_ref, total_ref, sums_ref, tokens, diagonal):
    rows = queries_ref.shape[1]
    chunk = chunk_of(rows)
    keys = kv_ref[:, :HD]
    values = kv_ref[:, HD:].T
    for start in range(0, rows, chunk):
        at = pl.ds(start, chunk)
        scores = jnp.dot(keys, queries_ref[:, at], preferred_element_type=jnp.float32)
        if diagonal:
            token = (start + lax.broadcasted_iota(jnp.int32, (1, chunk), 1)) % tokens
            key = lax.broadcasted_iota(jnp.int32, scores.shape, 0)
            scores = jnp.where(key <= token, scores, NEGATIVE)
        highest = jnp.max(scores, axis=0, keepdims=True)
        if not diagonal:
            before = highest_ref[:, at]
            highest = jnp.maximum(highest, before)
        shift = highest * EXP2_SCALE
        weights = jnp.exp2(scores * EXP2_SCALE - shift)
        total = jnp.sum(weights, axis=0, keepdims=True)
        sums = jnp.dot(values, weights.astype(jnp.bfloat16), preferred_element_type=jnp.float32)
        if not diagonal:
            factor = jnp.exp2(before * EXP2_SCALE - shift)
            total = total + total_ref[:, at] * factor
            sums = sums + sums_ref[:, at] * factor
        highest_ref[:, at] = highest
        total_ref[:, at] = total
        sums_ref[:, at] = sums


def add_earlier(place_ref, kv_refs, state, tokens):
    for i, kv_ref in enumerate(kv_refs):
        @pl.when(place_ref[1 + i] < place_ref[0])
        def _(kv_ref=kv_ref):
            add_block(kv_ref, *state, tokens, False)


def first_kernel(place_ref, query_ref, own_ref, *refs):
    kv_refs, (queries_ref, *state, stacked_ref) = refs[:-5], refs[-5:]
    tokens = query_ref.shape[0]
    for head in range(query_ref.shape[1] // HD):
        stacked_ref[pl.ds(head * tokens, tokens), :] = query_ref[:, pl.ds(head * HD, HD)]
    rows = stacked_ref.shape[0]
    chunk = chunk_of(rows)
    for start in range(0, rows, chunk):
        queries_ref[:, pl.ds(start, chunk)] = stacked_ref[pl.ds(start, chunk), :].T
    state = (queries_ref, *state)
    add_block(own_ref, *state, tokens, True)
    add_earlier(place_ref, kv_refs, state, tokens)


def next_kernel(tokens, place_ref, queries_ref, *refs):
    highest_in, total_in, sums_in = refs[:3]
    kv_refs, (highest_ref, total_ref, sums_ref) = refs[3:-3], refs[-3:]
    highest_ref[...] = highest_in[...]
    total_ref[...] = total_in[...]
    sums_ref[...] = sums_in[...]
    add_earlier(place_ref, kv_refs, (queries_ref, highest_ref, total_ref, sums_ref), tokens)


def last_kernel(tokens, parts, place_ref, queries_ref, *refs):
    highest_in, total_in, sums_in = refs[:3]
    kv_refs, w_ref = refs[3:-7], refs[-7]
    keep_ref, send_ref, highest_ref, total_ref, sums_ref, attended_ref = refs[-6:]
    highest_ref[...] = highest_in[...]
    total_ref[...] = total_in[...]
    sums_ref[...] = sums_in[...]
    add_earlier(place_ref, kv_refs, (queries_ref, highest_ref, total_ref, sums_ref), tokens)
    inverse = 1.0 / total_ref[...]
    done = (sums_ref[...] * inverse).astype(jnp.bfloat16).T
    for head in range(done.shape[0] // tokens):
        attended_ref[:, pl.ds(head * HD, HD)] = done[head * tokens : (head + 1) * tokens]
    me = place_ref[1 + len(kv_refs)]
    width = w_ref.shape[1] // parts
    for step in range(parts):
        step = (step + 1) % parts if parts > 1 else step
        columns = pl.ds(pl.multiple_of((me ^ step) * width, 128), width)
        partial = jnp.dot(attended_ref[...], w_ref[:, columns], preferred_element_type=jnp.float32)
        if step % 2:
            send_ref[step // 2] = partial.astype(send_ref.dtype)
        else:
            keep_ref[step // 2] = partial


def cost(rows, tokens, blocks, extra=0):
    return pl.CostEstimate(
        flops=4 * rows * tokens * blocks * HD + extra,
        bytes_accessed=rows * HD * 8 + blocks * tokens * HD * 4,
        transcendentals=rows * tokens * blocks,
    )


def on_device(query_rows, key_rows, value_rows, w_out):
    tokens, width = query_rows.shape
    rows = tokens * (width // HD)
    ctx, parts = lax.axis_size("ctx"), lax.axis_size("head")
    me, head = lax.axis_index("ctx"), lax.axis_index("head")
    f32 = functools.partial(jax.ShapeDtypeStruct, dtype=jnp.float32)
    state_shape = (f32((1, rows)), f32((1, rows)), f32((HD, rows)))
    pair = 2 if ctx % 2 == 0 else 1
    far = ctx // pair

    def places(sources, *more):
        return jnp.stack([me, *sources, *more]).astype(jnp.int32)

    def swap(block, distance):
        return lax.ppermute(block, "ctx", [(i, i ^ distance) for i in range(ctx)])

    own = pick((head * KVH // parts).astype(jnp.int32)[None], key_rows, value_rows)
    distances = [pair * step for step in range(1, far)]
    direct = [swap(own, distance) for distance in distances]
    beside = swap(own, 1)
    state = pl.pallas_call(
        first_kernel,
        out_shape=(jax.ShapeDtypeStruct((HD, rows), jnp.bfloat16), *state_shape),
        in_specs=[SMEM, VMEM, VMEM, VMEM],
        out_specs=(VMEM,) * 4,
        scratch_shapes=[pltpu.VMEM((rows, HD), jnp.bfloat16)],
        cost_estimate=cost(rows, tokens, 2),
        name="first",
    )(places([me ^ 1]), query_rows, own, beside)
    queries, state = state[0], state[1:]
    relayed = [swap(block, 1) for block in direct]

    def extend(state, blocks, sources):
        return pl.pallas_call(
            functools.partial(next_kernel, tokens),
            out_shape=state_shape,
            in_specs=[SMEM] + [VMEM] * (4 + len(blocks)),
            out_specs=(VMEM,) * 3,
            input_output_aliases={2: 0, 3: 1, 4: 2},
            cost_estimate=cost(rows, tokens, len(blocks)),
            name="next",
        )(places(sources), queries, *state, *blocks)

    group = 3
    calls = []
    for start in range(0, len(direct), group):
        calls.append((direct[start : start + group], [me ^ d for d in distances[start : start + group]]))
    for start in range(0, len(relayed), group):
        calls.append((relayed[start : start + group], [me ^ d ^ 1 for d in distances[start : start + group]]))
    for blocks, sources in calls[:-1]:
        state = extend(state, blocks, sources)
    blocks, sources = calls[-1]
    columns = w_out.shape[1] // parts
    keep, send = pl.pallas_call(
        functools.partial(last_kernel, tokens, parts),
        out_shape=(
            f32((parts // 2, tokens, columns)),
            jax.ShapeDtypeStruct((parts // 2, tokens, columns), jnp.bfloat16),
        ),
        in_specs=[SMEM] + [VMEM] * (5 + len(blocks)),
        out_specs=(VMEM,) * 2,
        scratch_shapes=[
            pltpu.VMEM((1, rows), jnp.float32),
            pltpu.VMEM((1, rows), jnp.float32),
            pltpu.VMEM((HD, rows), jnp.float32),
            pltpu.VMEM((tokens, width), jnp.bfloat16),
        ],
        cost_estimate=cost(rows, tokens, len(blocks), 2 * tokens * width * w_out.shape[1]),
        name="last",
    )(places(sources, head), queries, *state, *blocks, w_out)
    distance = 1
    while True:
        got = lax.ppermute(send, "head", [(i, i ^ distance) for i in range(parts)])
        if keep.shape[0] == 1:
            return (keep[0] + got[0]).astype(jnp.bfloat16)
        send = (keep[1::2] + got[1::2]).astype(jnp.bfloat16)
        keep = keep[0::2] + got[0::2]
        distance *= 2


def solution(mesh):
    placed = (P("ctx", "head"), P("ctx", None), P("ctx", None), P("head", None))
    return jax.shard_map(
        on_device, mesh=mesh, in_specs=placed, out_specs=P("ctx", "head"), check_vma=False
    )
```

```python
import functools
import math

import jax
import jax.numpy as jnp
from jax import lax
from jax.experimental import pallas as pl
from jax.experimental.pallas import tpu as pltpu
from jax.sharding import PartitionSpec as P

KVH = 4
HD = 128

NEGATIVE = -1e30
EXP2_SCALE = math.log2(math.e) / math.sqrt(HD)


VMEM = pl.BlockSpec(memory_space=pltpu.VMEM)
HBM = pl.BlockSpec(memory_space=pl.ANY)
GRANT = 16 << 20


def call(kernel, name, inputs, outputs, scratch=(), aliases=None, flops=0, exps=0, in_specs=None):
    moved = sum(math.prod(x.shape) * x.dtype.itemsize for x in (*inputs, *outputs))
    return pl.pallas_call(
        kernel,
        out_shape=tuple(outputs),
        in_specs=in_specs or [VMEM] * len(inputs),
        out_specs=(VMEM,) * len(outputs),
        scratch_shapes=list(scratch),
        input_output_aliases=aliases or {},
        cost_estimate=pl.CostEstimate(flops=flops, bytes_accessed=moved, transcendentals=exps),
        compiler_params=pltpu.CompilerParams(vmem_limit_bytes=GRANT),
        name=name,
    )(*inputs)


def chunk_of(rows):
    return 256 if rows % 256 == 0 else 128 if rows % 128 == 0 else rows


def pick_kernel(key_ref, value_ref, out_ref, sems):
    kv_head = lax.axis_index("head") * KVH // lax.axis_size("head")
    column = pl.multiple_of(kv_head * HD, HD)
    copies = [
        pltpu.make_async_copy(
            ref.at[:, pl.ds(column, HD)], out_ref.at[:, pl.ds(i * HD, HD)], sems.at[i]
        )
        for i, ref in enumerate((key_ref, value_ref))
    ]
    for copy in copies:
        copy.start()
    for copy in copies:
        copy.wait()


def add_block(kv_ref, queries_ref, highest_ref, total_ref, sums_ref, tokens, first):
    rows = queries_ref.shape[1]
    chunk = chunk_of(rows)
    keys = kv_ref[:, :HD]
    values = kv_ref[:, HD:].T

    def score(start):
        queries = queries_ref[:, pl.ds(start, chunk)]
        return jnp.dot(keys, queries, preferred_element_type=jnp.float32)

    def weigh(start, scores):
        at = pl.ds(start, chunk)
        if first:
            token = (start + lax.broadcasted_iota(jnp.int32, (1, chunk), 1)) % tokens
            key = lax.broadcasted_iota(jnp.int32, scores.shape, 0)
            scores = jnp.where(key <= token, scores, NEGATIVE)
        highest = jnp.max(scores, axis=0, keepdims=True)
        if not first:
            before = highest_ref[:, at]
            highest = jnp.maximum(highest, before)
        shift = highest * EXP2_SCALE
        weights = jnp.exp2(scores * EXP2_SCALE - shift)
        total = jnp.sum(weights, axis=0, keepdims=True)
        factor = None
        if not first:
            factor = jnp.exp2(before * EXP2_SCALE - shift)
            total = total + total_ref[:, at] * factor
        highest_ref[:, at] = highest
        total_ref[:, at] = total
        return start, weights.astype(jnp.bfloat16), factor

    def gather(start, weights, factor):
        at = pl.ds(start, chunk)
        sums = jnp.dot(values, weights, preferred_element_type=jnp.float32)
        if not first:
            sums = sums + sums_ref[:, at] * factor
        sums_ref[:, at] = sums

    scores, weighed = score(0), None
    for start in range(0, rows, chunk):
        following = score(start + chunk) if start + chunk < rows else None
        done = weigh(start, scores)
        if weighed is not None:
            gather(*weighed)
        weighed, scores = done, following
    gather(*weighed)


def first_kernel(query_ref, own_ref, queries_ref, highest_ref, total_ref, sums_ref, stacked_ref):
    tokens = query_ref.shape[0]
    for head in range(query_ref.shape[1] // HD):
        stacked_ref[pl.ds(head * tokens, tokens), :] = query_ref[:, pl.ds(head * HD, HD)]
    rows = stacked_ref.shape[0]
    chunk = chunk_of(rows)
    for start in range(0, rows, chunk):
        queries_ref[:, pl.ds(start, chunk)] = stacked_ref[pl.ds(start, chunk), :].T
    add_block(own_ref, queries_ref, highest_ref, total_ref, sums_ref, tokens, True)


def add_if_earlier(offset, kv_ref, queries_ref, given, state, tokens):
    for old, new in zip(given, state):
        new[...] = old[...]
    me = lax.axis_index("ctx")

    @pl.when((me ^ offset) < me)
    def _():
        add_block(kv_ref, queries_ref, *state, tokens, False)


def next_kernel(offset, tokens, queries_ref, *refs):
    add_if_earlier(offset, refs[3], queries_ref, refs[:3], refs[4:], tokens)


def project(attended_ref, w_ref, steps, parts, out_ref):
    width = w_ref.shape[1] // parts
    me = lax.axis_index("head")
    for i, step in enumerate(steps):
        columns = pl.ds(pl.multiple_of((me ^ step) * width, 128), width)
        partial = jnp.dot(attended_ref[...], w_ref[:, columns], preferred_element_type=jnp.float32)
        out_ref[i] = partial.astype(out_ref.dtype)


def last_kernel(offset, tokens, steps, parts, queries_ref, *refs):
    given, kv_ref, w_ref, attended_ref, out_ref, state = refs[:3], refs[3], refs[4], refs[5], refs[6], refs[7:]
    add_if_earlier(offset, kv_ref, queries_ref, given, state, tokens)
    _, total_ref, sums_ref = state
    done = (sums_ref[...] * (1.0 / total_ref[...])).astype(jnp.bfloat16).T
    for head in range(done.shape[0] // tokens):
        attended_ref[:, pl.ds(head * HD, HD)] = done[head * tokens : (head + 1) * tokens]
    project(attended_ref, w_ref, steps, parts, out_ref)


def project_kernel(steps, parts, attended_ref, w_ref, out_ref):
    project(attended_ref, w_ref, steps, parts, out_ref)


def join_kernel(*refs):
    out_ref = refs[-1]
    total = refs[0][...]
    for ref in refs[1:-1]:
        total = total + ref[...]
    out_ref[...] = total.astype(out_ref.dtype)


def on_device(query_rows, key_rows, value_rows, w_out):
    tokens, width = query_rows.shape
    rows = tokens * (width // HD)
    ctx, parts = lax.axis_size("ctx"), lax.axis_size("head")
    f32 = functools.partial(jax.ShapeDtypeStruct, dtype=jnp.float32)
    bf16 = functools.partial(jax.ShapeDtypeStruct, dtype=jnp.bfloat16)
    state_shape = (f32((1, rows)), f32((1, rows)), f32((HD, rows)))
    work = dict(flops=4 * rows * tokens * HD, exps=rows * tokens)
    columns = w_out.shape[1] // parts

    def swap(block, axis, distance):
        return lax.ppermute(block, axis, [(i, i ^ distance) for i in range(lax.axis_size(axis))])

    (own,) = call(
        pick_kernel,
        "pick",
        (key_rows, value_rows),
        (bf16((tokens, 2 * HD)),),
        scratch=(pltpu.SemaphoreType.DMA((2,)),),
        in_specs=[HBM, HBM],
    )
    distances = list(range(2, ctx, 2))
    direct = [(distance, swap(own, "ctx", distance)) for distance in distances]
    beside = [(1, swap(own, "ctx", 1))]
    relayed = [(distance ^ 1, swap(block, "ctx", 1)) for distance, block in direct]
    queries, *state = call(
        first_kernel,
        "first",
        (query_rows, own),
        (bf16((HD, rows)), *state_shape),
        scratch=(pltpu.VMEM((rows, HD), jnp.bfloat16),),
        **work,
    )
    blocks = beside + direct + relayed
    for offset, block in blocks[:-1]:
        state = call(
            functools.partial(next_kernel, offset, tokens),
            f"next{offset}",
            (queries, *state, block),
            state_shape,
            aliases={1: 0, 2: 1, 3: 2},
            **work,
        )
    offset, block = blocks[-1]
    half = parts // 2
    per_block = 2 * tokens * width * columns

    def product(steps, kind, name):
        return call(
            functools.partial(project_kernel, steps, parts),
            name,
            (attended, w_out),
            (kind((len(steps), tokens, columns)),),
            flops=per_block * len(steps),
        )[0]

    def join(name, kind, *terms):
        return call(join_kernel, name, terms, (kind(terms[0].shape),))[0]

    def fold(keep, send, name):
        distance = 1
        while True:
            got = swap(send, "head", distance)
            if keep.shape[0] == 1:
                return keep, got
            keep = join(name, f32, keep, got)
            keep, send = keep[0::2], keep[1::2].astype(jnp.bfloat16)
            distance *= 2

    top_send, top_keep = range(half + 1, parts, 2), range(half, parts, 2)
    attended, send = call(
        functools.partial(last_kernel, offset, tokens, top_send, parts),
        "last",
        (queries, *state, block, w_out),
        (bf16((tokens, width)), bf16((len(top_send), tokens, columns))),
        scratch=[pltpu.VMEM(s.shape, s.dtype) for s in state_shape],
        flops=work["flops"] + per_block * len(top_send),
        exps=work["exps"],
    )
    keep, got = fold(product(top_keep, f32, "top"), send, "topfold")
    far = swap(join("topsum", bf16, keep, got), "head", half)
    keep, got = fold(
        product(range(0, half, 2), f32, "low"), product(range(1, half, 2), bf16, "lowsend"), "lowfold"
    )
    return join("sum", bf16, keep, got, far)[0]


def solution(mesh):
    placed = (P("ctx", "head"), P("ctx", None), P("ctx", None), P("head", None))
    return jax.shard_map(
        on_device, mesh=mesh, in_specs=placed, out_specs=P("ctx", "head"), check_vma=False
    )
```

```python
import functools
import math

import jax
import jax.numpy as jnp
from jax import lax
from jax.experimental import pallas as pl
from jax.experimental.pallas import tpu as pltpu
from jax.sharding import PartitionSpec as P


KVH = 4
HD = 128

NEGATIVE = -1e30
EXP2_SCALE = math.log2(math.e) / math.sqrt(HD)


VMEM = pl.BlockSpec(memory_space=pltpu.VMEM)
HBM = pl.BlockSpec(memory_space=pltpu.HBM)
GRANT = 16 << 20


def call(kernel, inputs, outputs, scratch=(), aliases=None, flops=0, exps=0, in_specs=None):
    moved = sum(math.prod(x.shape) * x.dtype.itemsize for x in (*inputs, *outputs))
    return pl.pallas_call(
        kernel,
        out_shape=tuple(outputs),
        in_specs=in_specs or [VMEM] * len(inputs),
        out_specs=(VMEM,) * len(outputs),
        scratch_shapes=list(scratch),
        input_output_aliases=aliases or {},
        cost_estimate=pl.CostEstimate(flops=flops, bytes_accessed=moved, transcendentals=exps),
        compiler_params=pltpu.CompilerParams(vmem_limit_bytes=GRANT),
    )(*inputs)


def chunk_of(rows):
    return next(size for size in (512, 256, 128, rows) if rows % size == 0)


def pick_kernel(key_ref, value_ref, query_ref, out_ref, stacked_ref, sems):
    kv_head = lax.axis_index("head") * KVH // lax.axis_size("head")
    column = pl.multiple_of(kv_head * HD, HD)
    tokens = query_ref.shape[0]
    moves = [
        (ref.at[:, pl.ds(column, HD)], out_ref.at[:, pl.ds(i * HD, HD)])
        for i, ref in enumerate((key_ref, value_ref))
    ]
    for head in range(query_ref.shape[1] // HD):
        moves.append((query_ref.at[:, pl.ds(head * HD, HD)], stacked_ref.at[pl.ds(head * tokens, tokens)]))
    copies = [pltpu.make_async_copy(*move, sems.at[i]) for i, move in enumerate(moves)]
    for copy in copies:
        copy.start()
    for copy in copies:
        copy.wait()


def add_blocks(kv_refs, allowed, queries_ref, given, state, tokens):
    highest_ref, total_ref, sums_ref = state
    rows = queries_ref.shape[1]
    chunk = chunk_of(rows)
    keys = [ref[:, :HD] for ref in kv_refs]
    values = [ref[:, HD:].T for ref in kv_refs]

    def score(start):
        queries = queries_ref[:, pl.ds(start, chunk)]
        return [jnp.dot(key, queries, preferred_element_type=jnp.float32) for key in keys]

    def weigh(start, scores):
        at = pl.ds(start, chunk)
        if given is None:
            token = (start + lax.broadcasted_iota(jnp.int32, (1, chunk), 1)) % tokens
            key = lax.broadcasted_iota(jnp.int32, scores[0].shape, 0)
            scores = [jnp.where(key <= token, scores[0], NEGATIVE)]
            highest = jnp.max(scores[0], axis=0, keepdims=True)
        else:
            before = given[0][:, at]
            highest = before
            for score, allow in zip(scores, allowed):
                top = jnp.max(score, axis=0, keepdims=True)
                highest = jnp.maximum(highest, jnp.where(allow, top, NEGATIVE))
        shift = highest * EXP2_SCALE
        factor, total = None, None
        if given is not None:
            factor = jnp.exp2(before * EXP2_SCALE - shift)
            total = given[1][:, at] * factor
        weights = []
        for score, allow in zip(scores, allowed):
            own_shift = shift if allow is True else jnp.where(allow, shift, -NEGATIVE)
            weight = jnp.exp2(score * EXP2_SCALE - own_shift)
            added = jnp.sum(weight, axis=0, keepdims=True)
            total = added if total is None else total + added
            weights.append(weight.astype(jnp.bfloat16))
        highest_ref[:, at] = highest
        total_ref[:, at] = total
        return start, weights, factor

    def gather(start, weights, factor):
        at = pl.ds(start, chunk)
        sums = sum(
            jnp.dot(value, weight, preferred_element_type=jnp.float32)
            for value, weight in zip(values, weights)
        )
        if given is not None:
            sums = sums + given[2][:, at] * factor
        sums_ref[:, at] = sums

    scores, weighed = score(0), None
    for start in range(0, rows, chunk):
        following = score(start + chunk) if start + chunk < rows else None
        done = weigh(start, scores)
        if weighed is not None:
            gather(*weighed)
        weighed, scores = done, following
    gather(*weighed)


def first_kernel(tokens, stacked_ref, own_ref, queries_ref, *state):
    rows = stacked_ref.shape[0]
    chunk = chunk_of(rows)
    for start in range(0, rows, chunk):
        queries_ref[:, pl.ds(start, chunk)] = stacked_ref[pl.ds(start, chunk), :].T
    add_blocks([own_ref], [True], queries_ref, None, state, tokens)


def add_earlier(offsets, kv_refs, queries_ref, given, state, tokens):
    me = lax.axis_index("ctx")
    allowed = [(me ^ offset) < me for offset in offsets]
    some = functools.reduce(jnp.logical_or, allowed)

    @pl.when(some)
    def _():
        add_blocks(kv_refs, allowed, queries_ref, given, state, tokens)

    @pl.when(jnp.logical_not(some))
    def _():
        for old, new in zip(given, state):
            new[...] = old[...]


def next_kernel(offsets, tokens, queries_ref, *refs):
    add_earlier(offsets, refs[3:-3], queries_ref, refs[:3], refs[-3:], tokens)


def project(attended_ref, w_ref, steps, parts, out_ref):
    width = w_ref.shape[1] // parts
    me = lax.axis_index("head")
    for i, step in enumerate(steps):
        columns = pl.ds(pl.multiple_of((me ^ step) * width, 128), width)
        partial = jnp.dot(attended_ref[...], w_ref[:, columns], preferred_element_type=jnp.float32)
        out_ref[i] = partial.astype(out_ref.dtype)


def last_kernel(offsets, tokens, steps, parts, queries_ref, *refs):
    given, kv_refs, state = refs[:3], refs[3:-6], refs[-3:]
    w_ref, attended_ref, out_ref = refs[-6:-3]
    add_earlier(offsets, kv_refs, queries_ref, given, state, tokens)
    _, total_ref, sums_ref = state
    done = (sums_ref[...] * (1.0 / total_ref[...])).astype(jnp.bfloat16).T
    for head in range(done.shape[0] // tokens):
        attended_ref[:, pl.ds(head * HD, HD)] = done[head * tokens : (head + 1) * tokens]
    project(attended_ref, w_ref, steps, parts, out_ref)


def project_kernel(steps, parts, attended_ref, w_ref, out_ref):
    project(attended_ref, w_ref, steps, parts, out_ref)


def join_kernel(*refs):
    out_ref = refs[-1]
    total = refs[0][...]
    for ref in refs[1:-1]:
        total = total + ref[...]
    out_ref[...] = total.astype(out_ref.dtype)


def on_device(query_rows, key_rows, value_rows, w_out):
    tokens, width = query_rows.shape
    rows = tokens * (width // HD)
    ctx, parts = lax.axis_size("ctx"), lax.axis_size("head")
    f32 = functools.partial(jax.ShapeDtypeStruct, dtype=jnp.float32)
    bf16 = functools.partial(jax.ShapeDtypeStruct, dtype=jnp.bfloat16)
    state_shape = (f32((1, rows)), f32((1, rows)), f32((HD, rows)))
    columns = w_out.shape[1] // parts

    def work(count, more=0):
        return dict(flops=4 * rows * tokens * HD * count + more, exps=rows * tokens * count)

    def swap(block, axis, distance):
        return lax.ppermute(block, axis, [(i, i ^ distance) for i in range(lax.axis_size(axis))])

    own, stacked = call(
        pick_kernel,
        tuple(pltpu.with_memory_space_constraint(x, pltpu.HBM) for x in (key_rows, value_rows, query_rows)),
        (bf16((tokens, 2 * HD)), bf16((rows, HD))),
        scratch=(pltpu.SemaphoreType.DMA((2 + width // HD,)),),
        in_specs=[HBM] * 3,
    )
    near, far = offsets_of(ctx)
    direct = {d: swap(own, "ctx", d) for d in far + near}
    relayed = {d ^ step: swap(direct[d], "ctx", step) for d in far for step in near}
    blocks = {**direct, **relayed}
    queries, *state = call(
        functools.partial(first_kernel, tokens), (stacked, own), (bf16((HD, rows)), *state_shape), **work(1)
    )
    groups = groups_of(ctx)
    for group in groups[:-1]:
        state = call(
            functools.partial(next_kernel, group, tokens),
            (queries, *state, *(blocks[d] for d in group)),
            state_shape,
            aliases={1: 0, 2: 1, 3: 2},
            **work(len(group)),
        )
    half = parts // 2
    per_block = 2 * tokens * width * columns

    def product(steps, kind):
        return call(
            functools.partial(project_kernel, steps, parts),
            (attended, w_out),
            (kind((len(steps), tokens, columns)),),
            flops=per_block * len(steps),
        )[0]

    def join(kind, *terms):
        return call(join_kernel, terms, (kind(terms[0].shape),))[0]

    def fold(keep, send):
        distance = 1
        while True:
            got = swap(send, "head", distance)
            if keep.shape[0] == 1:
                return keep, got
            keep = join(f32, keep, got)
            keep, send = keep[0::2], keep[1::2].astype(jnp.bfloat16)
            distance *= 2

    top_send, top_keep = range(half + 1, parts, 2), range(half, parts, 2)
    attended, send = call(
        functools.partial(last_kernel, groups[-1], tokens, top_send, parts),
        (queries, *state, *(blocks[d] for d in groups[-1]), w_out),
        (bf16((tokens, width)), bf16((len(top_send), tokens, columns))),
        scratch=[pltpu.VMEM(s.shape, s.dtype) for s in state_shape],
        **work(len(groups[-1]), per_block * len(top_send)),
    )
    keep, got = fold(product(top_keep, f32), send)
    far = swap(join(bf16, keep, got), "head", half)
    keep, got = fold(product(range(0, half, 2), f32), product(range(1, half, 2), bf16))
    return join(bf16, keep, got, far)[0]


def offsets_of(ctx):
    return [d for d in (3, 1, 2) if d < ctx], list(range(ctx - 4, 0, -4))


def groups_of(ctx):
    near, far = offsets_of(ctx)
    order = near + [block for d in far for block in (d, d ^ 3, d ^ 1, d ^ 2)]
    groups = [order[i : i + 2] for i in range(0, len(order), 2)]
    groups = [group for group in groups if group]
    return groups[:-1] + [part for part in (groups[-1][:-1], groups[-1][-1:]) if part]


def solution(mesh):
    placed = (P("ctx", "head"), P("ctx", None), P("ctx", None), P("head", None))

    return jax.shard_map(on_device, mesh=mesh, in_specs=placed, out_specs=P("ctx", "head"), check_vma=False)
```
